32 devices in a mesh: dp: 2 (over core), sx: 2 (over x), syz: 8 (over z, y).
Axes of the slice: x: 2, y: 2, z: 4, core: 2. Of those that a mesh axis runs over, the one named last changes fastest.
Arguments:
- volume: bfloat16 [2, 16, 32, 128, 256], P('dp', 'sx', 'syz'), may hold values from -80 to 80
- kernel: bfloat16 [3, 3, 3, 32, 256], replicated, may hold values from -1.36082763 to 1.36082763
Outputs:
- whitened: bfloat16 [2, 16, 32, 128, 256], P('dp', 'sx', 'syz')
The draws below stay inside these ranges and needn't reach their ends.
All inputs are finite; a program needn't handle non-finite values.
Results may differ from the reference program's by a relative error of at most 0.006.
Values may be sent and summed in bfloat16 or wider, within the bound.
A program may use at most 128 MiB of HBM per device.

```python
import jax
import jax.numpy as jnp
from jax import lax

NZ = 128
CHAN = 256
GROUPS = 8
WGROUPS = 2
STEPS = 5
GC = 32
WG = 128
SAMPLES = 2
NX = 16
NY = 32


def draw_volume(key, part):
    keys = jax.random.split(key, 2)
    shape = (SAMPLES, NX, NY, NZ, CHAN)
    places_x = (jnp.arange(NX, dtype=jnp.float32) / NX).reshape(1, NX, 1, 1, 1)
    places_y = (jnp.arange(NY, dtype=jnp.float32) / NY).reshape(1, 1, NY, 1, 1)
    rough = jnp.exp(jax.random.uniform(keys[1], shape, jnp.float32, -0.7, 0.7))
    base = jnp.clip(jax.random.normal(keys[0], shape, jnp.float32), -4.0, 4.0)
    values = base * 10.0 ** (0.5 * (places_x + places_y)) * rough
    return jnp.clip(values, -80.0, 80.0).astype(jnp.bfloat16)


def draw_kernel(key, part):
    keys = jax.random.split(key, 2)
    base = jnp.clip(jax.random.normal(keys[0], (3, 3, 3, GC, CHAN), jnp.float32), -4.0, 4.0)
    column_scale = jnp.exp(jax.random.uniform(keys[1], (1, 1, 1, 1, CHAN), jnp.float32, 0.0, 2.302585))
    return (base * column_scale / (27.0 * GC) ** 0.5).astype(jnp.bfloat16)


def setup_inputs(seed: int = 0) -> dict:
    key_of = jax.random.split(jax.random.key(seed), 3)
    return {
        "volume": draw_volume(jax.random.fold_in(key_of[2], 71), 0),
        "kernel": draw_kernel(jax.random.fold_in(key_of[2], 71), 0),
    }


highest = lax.Precision.HIGHEST
epsilon = 1e-05

def whiten_matrix(covariance):
    identity = jnp.eye(covariance.shape[-1], dtype=jnp.float32)
    shifted = covariance + epsilon * identity
    frobenius = jnp.sqrt(lax.optimization_barrier(jnp.sum(shifted * shifted, axis=(1, 2))))[:, None, None]
    iterate_y = shifted / frobenius
    iterate_z = jnp.broadcast_to(identity, shifted.shape)
    for number in range(STEPS):
        factor = 1.5 * identity - 0.5 * jnp.einsum('gab,gbc->gac', iterate_z, iterate_y, precision=highest)
        iterate_y = jnp.einsum('gab,gbc->gac', iterate_y, factor, precision=highest)
        iterate_z = jnp.einsum('gab,gbc->gac', factor, iterate_z, precision=highest)
    return iterate_z / jnp.sqrt(frobenius)

def convolve(sample, kernel):
    result = lax.conv_general_dilated(sample[None].astype(jnp.float32), kernel.astype(jnp.float32), (1, 1, 1), ((1, 1), (1, 1), (1, 1)), dimension_numbers=('NDHWC', 'DHWIO', 'NDHWC'), feature_group_count=GROUPS, precision=highest)
    return result[0].astype(jnp.bfloat16)

def reference(volume, kernel):
    hidden = lax.map(lambda sample: convolve(sample, kernel), volume)
    voxels = hidden.reshape(-1, WGROUPS, WG)
    counts = float(voxels.shape[0])
    wide_voxels = voxels.astype(jnp.float32)
    sum_first = lax.optimization_barrier(jnp.sum(wide_voxels, axis=0))
    sum_second = jnp.einsum('nga,ngb->gab', wide_voxels, wide_voxels, precision=highest)
    average = sum_first / counts
    covariance = sum_second / counts - average[:, :, None] * average[:, None, :]
    whitener = whiten_matrix(covariance)
    whitener_b = whitener.astype(jnp.bfloat16).astype(jnp.float32)
    shift = lax.optimization_barrier(jnp.sum(whitener_b * average[:, None, :], axis=2))
    result = jnp.einsum('nga,gba->ngb', wide_voxels, whitener_b, precision=highest) - shift
    return result.astype(jnp.bfloat16).reshape(volume.shape)
```

```python
import functools

import jax
import jax.numpy as jnp
from jax import lax
from jax.experimental import pallas as pl
from jax.experimental.pallas import tpu as pltpu
from jax.sharding import PartitionSpec as P

WGROUPS = 2
STEPS = 5
epsilon = 1e-05
highest = lax.Precision.HIGHEST
MESH = pl.DeviceIdType.MESH
F32 = jnp.float32
BF16 = jnp.bfloat16
OTHERS = ((-1, 0), (1, 0), (-1, -1), (-1, 1), (1, -1), (1, 1))


def fma(a, b):
    return jnp.dot(a, b, preferred_element_type=F32)


def fdot(a, b):
    return jnp.dot(a, b, precision=highest, preferred_element_type=F32)


def main_kernel(
    sizes, stages, parts, whole_count,
    v_ref, k_ref, hid_out, white_ref, shift_ref,
    xs, wd, acc, hid, gram, red, got, give, got_pair, fin, got_fin,
    load_sem, store_sem, send_y, recv_y, send_o, recv_o,
    pair_send, pair_recv, tree_send, tree_recv,
):
    nx, ny = sizes
    X, Y, Z, C = v_ref.shape[1:]
    GC = k_ref.shape[1]
    WG = C // WGROUPS
    me_d = lax.axis_index("dp")
    me_x = lax.axis_index("sx")
    me_y = lax.axis_index("syz")

    def flip(axis, bit):
        me = lax.axis_index(axis)
        return {axis: me + bit - 2 * bit * ((me // bit) % 2)}

    def there(dx, dy):
        ok = None
        for d, me, n in ((dx, me_x, nx), (dy, me_y, ny)):
            if d:
                t = (me >= 1) if d < 0 else (me < n - 1)
                ok = t if ok is None else ok & t
        return ok

    def target(dx, dy):
        return (me_d, me_x + dx, me_y + dy)

    load = pltpu.make_async_copy(
        v_ref.at[0], xs.at[pl.ds(1, X), pl.ds(1, Y), :, pl.ds(C, C)], load_sem)
    load.start()

    barrier = pltpu.get_barrier_semaphore()
    near = ((0, -1), (0, 1)) + OTHERS
    for dx, dy in near:
        @pl.when(there(dx, dy))
        def _(dx=dx, dy=dy):
            pl.semaphore_signal(barrier, inc=1, device_id=target(dx, dy), device_id_type=MESH)
    far = [flip("dp", 1)] + [flip(a, b) for a, b in stages]
    for who in far:
        pl.semaphore_signal(barrier, inc=1, device_id=who, device_id_type=MESH)
    has_x = [jnp.where(there(d, 0), 1, 0) for d in (-1, 1)]
    has_y = [jnp.where(there(0, d), 1, 0) for d in (-1, 1)]
    around = (1 + has_x[0] + has_x[1]) * (1 + has_y[0] + has_y[1]) - 1
    pl.semaphore_wait(barrier, around + len(far))

    def span(d, n):
        if d == 0:
            return pl.ds(0, n), pl.ds(1, n)
        if d < 0:
            return pl.ds(0, 1), pl.ds(n + 1, 1)
        return pl.ds(n - 1, 1), pl.ds(0, 1)

    def halo(dx, dy, send, recv):
        sx, tx = span(dx, X)
        sy, ty = span(dy, Y)
        return pltpu.make_async_remote_copy(
            src_ref=v_ref.at[0, sx, sy],
            dst_ref=xs.at[tx, ty, :, pl.ds(C, C)],
            send_sem=send, recv_sem=recv,
            device_id=target(dx, dy), device_id_type=MESH)

    halos = [(0, -1, send_y.at[0], recv_y.at[0]), (0, 1, send_y.at[1], recv_y.at[1])]
    halos += [(dx, dy, send_o.at[i], recv_o.at[i]) for i, (dx, dy) in enumerate(OTHERS)]
    for dx, dy, s, r in halos:
        @pl.when(there(dx, dy))
        def _(dx=dx, dy=dy, s=s, r=r):
            halo(dx, dy, s, r).start()

        @pl.when(jnp.logical_not(there(-dx, -dy)))
        def _(dx=dx, dy=dy):
            tx, ty = span(dx, X)[1], span(dy, Y)[1]
            xs[tx, ty, :, pl.ds(C, C)] = jnp.zeros((tx.size, ty.size, Z, C), BF16)

    lanes = lax.broadcasted_iota(jnp.int32, (GC, C), 1) // GC

    @pl.loop(0, k_ref.shape[0])
    def _(t):
        w = k_ref[t].astype(F32)
        for g in range(C // GC):
            wd[t, pl.ds(g * GC, GC), :] = jnp.where(lanes == g, w, 0.0).astype(BF16)

    rows = lax.broadcasted_iota(jnp.int32, (Z, C), 0)

    def shifted(px, py):
        v = xs[px, py, :, pl.ds(C, C)].astype(F32)
        xs[px, py, :, pl.ds(0, C)] = jnp.where(rows == 0, 0.0, pltpu.roll(v, 1, 0)).astype(BF16)
        xs[px, py, :, pl.ds(2 * C, C)] = jnp.where(
            rows == Z - 1, 0.0, pltpu.roll(v, Z - 1, 0)).astype(BF16)

    load.wait()

    @pl.loop(1, X + 1)
    def _(px):
        for py in range(1, Y + 1):
            shifted(px, py)

    def weight(a, b):
        return wd[pl.ds(((a + 1) * 3 + b + 1) * 3, 3)].reshape(3 * C, C)

    def inner(px, y0, n):
        return xs[px, pl.ds(y0, n)].reshape(n * Z, 3 * C)

    def plane(x, offsets):
        full = sum(fma(inner(x + 1 + a, 1, Y), weight(a, 0)) for a in offsets)
        acc[x] = full
        if Y > 1:
            m = (Y - 1) * Z
            acc[x, pl.ds(Z, m)] += sum(fma(inner(x + 1 + a, 1, Y - 1), weight(a, -1)) for a in offsets)
            acc[x, pl.ds(0, m)] += sum(fma(inner(x + 1 + a, 2, Y - 1), weight(a, 1)) for a in offsets)

    if X == 1:
        plane(0, (0,))
    else:
        plane(0, (0, 1))
        if X > 2:
            @pl.loop(1, X - 1)
            def _(x):
                plane(x, (-1, 0, 1))
        plane(X - 1, (-1, 0))

    for dx, dy, s, r in halos:
        @pl.when(there(-dx, -dy))
        def _(dx=dx, dy=dy, s=s, r=r):
            halo(dx, dy, s, r).wait_recv()

    @pl.loop(0, X + 2)
    def _(px):
        for py in (0, Y + 1):
            shifted(px, py)

    @pl.loop(1, Y + 1)
    def _(py):
        for px in (0, X + 1):
            shifted(px, py)

    for px, x, a in ((0, 0, -1), (X + 1, X - 1, 1)):
        acc[x] += sum(fma(inner(px, b + 1, Y), weight(a, b)) for b in (-1, 0, 1))
    for py, y, b in ((0, 0, -1), (Y + 1, Y - 1, 1)):
        for a in (-1, 0, 1):
            x0, n = (0, X) if a == 0 else ((1, X - 1) if a < 0 else (0, X - 1))
            if n:
                lhs = xs[pl.ds(x0 + 1 + a, n), py].reshape(n * Z, 3 * C)
                acc[pl.ds(x0, n), pl.ds(y * Z, Z)] += fma(lhs, weight(a, b)).reshape(n, Z, C)

    gram[...] = jnp.zeros_like(gram)

    @pl.loop(0, X)
    def _(x):
        h = acc[x].astype(BF16)
        hid[x] = h
        gram[pl.ds(0, C)] += lax.dot_general(
            h, h, (((0,), (0,)), ((), ())), preferred_element_type=F32)
        gram[pl.ds(C, 8)] += jnp.sum(h.astype(F32).reshape(Y * Z // 8, 8, C), axis=0)

    store = pltpu.make_async_copy(hid, hid_out, store_sem)
    store.start()

    mine = me_d == 0
    low = gram[pl.ds(0, WG), pl.ds(0, WG)]
    high = gram[pl.ds(WG, WG), pl.ds(WG, WG)]
    low_sum = gram[pl.ds(C, 8), pl.ds(0, WG)]
    high_sum = gram[pl.ds(C, 8), pl.ds(WG, WG)]
    give[pl.ds(0, WG)] = jnp.where(mine, high, low)
    give[pl.ds(WG, 8)] = jnp.where(mine, high_sum, low_sum)
    pair = flip("dp", 1)
    swap = pltpu.make_async_remote_copy(
        src_ref=give, dst_ref=got_pair, send_sem=pair_send.at[0], recv_sem=pair_recv.at[0],
        device_id=pair, device_id_type=MESH)
    swap.start()
    own = jnp.where(mine, low, high)
    own_sum = jnp.where(mine, low_sum, high_sum)
    swap.wait()
    red[0, pl.ds(0, WG)] = own + got_pair[pl.ds(0, WG)]
    red[0, pl.ds(WG, 8)] = own_sum + got_pair[pl.ds(WG, 8)]

    count = len(stages)

    def leg(step, stream):
        axis, bit = stages[(step + stream) % count]
        part = pl.ds(*parts[stream])
        return pltpu.make_async_remote_copy(
            src_ref=red.at[step, part], dst_ref=got.at[step, part],
            send_sem=tree_send.at[step, stream], recv_sem=tree_recv.at[step, stream],
            device_id=flip(axis, bit), device_id_type=MESH)

    for step in range(count):
        for stream in range(len(parts)):
            leg(step, stream).start()
        for stream in range(len(parts)):
            leg(step, stream).wait_recv()
            part = pl.ds(*parts[stream])
            red[step + 1, part] = red[step, part] + got[step, part]

    average = jnp.sum(red[count, pl.ds(WG, 8)], axis=0, keepdims=True) / whole_count
    across = jnp.broadcast_to(average, (WG, WG))
    down = across.T
    covariance = red[count, pl.ds(0, WG)] / whole_count - down * across
    identity = jnp.where(
        lax.broadcasted_iota(jnp.int32, (WG, WG), 0) == lax.broadcasted_iota(jnp.int32, (WG, WG), 1),
        1.0, 0.0).astype(F32)
    moved = covariance + epsilon * identity
    square = jnp.sum(jnp.sum(moved * moved, axis=1, keepdims=True), axis=0, keepdims=True)
    frobenius = jnp.sqrt(square)
    y = moved / frobenius
    z = None
    for number in range(STEPS):
        p = 1.5 * identity - 0.5 * (y if z is None else fdot(z, y))
        if number < STEPS - 1:
            y = fdot(y, p)
        z = p if z is None else fdot(p, z)
    whitener = z / jnp.sqrt(frobenius)
    turned = whitener.T.astype(BF16).astype(F32)
    fin[pl.ds(0, WG)] = turned
    fin[pl.ds(WG, 8)] = jnp.broadcast_to(jnp.sum(turned * down, axis=0, keepdims=True), (8, WG))
    swap = pltpu.make_async_remote_copy(
        src_ref=fin, dst_ref=got_fin, send_sem=pair_send.at[1], recv_sem=pair_recv.at[1],
        device_id=pair, device_id_type=MESH)
    swap.start()
    own = fin[...]
    swap.wait()
    other = got_fin[...]
    first = jnp.where(mine, own, other)
    second = jnp.where(mine, other, own)
    white_ref[...] = jnp.zeros_like(white_ref)
    white_ref[pl.ds(0, WG), pl.ds(0, WG)] = first[:WG].astype(BF16)
    white_ref[pl.ds(WG, WG), pl.ds(WG, WG)] = second[:WG].astype(BF16)
    shift_ref[:, pl.ds(0, WG)] = first[WG:]
    shift_ref[:, pl.ds(WG, WG)] = second[WG:]

    store.wait()
    for step in range(count):
        for stream in range(len(parts)):
            leg(step, stream).wait_send()
    for dx, dy, s, r in halos:
        @pl.when(there(dx, dy))
        def _(dx=dx, dy=dy, s=s, r=r):
            halo(dx, dy, s, r).wait_send()


def apply_kernel(h_ref, w_ref, s_ref, o_ref):
    X, M, C = h_ref.shape
    result = fma(h_ref[...].reshape(X * M, C), w_ref[...]) - s_ref[0:1, :]
    o_ref[...] = result.astype(BF16).reshape(o_ref.shape)


def on_device(sizes, volume, kernel):
    nd, nx, ny = sizes
    X, Y, Z, C = volume.shape[1:]
    GC = kernel.shape[3]
    WG = C // WGROUPS
    stages = []
    for axis, n in (("sx", nx), ("syz", ny)):
        bit = 1
        while bit < n:
            stages.append((axis, bit))
            bit *= 2
    streams = min(4, len(stages))
    blocks = (WG + 8) // 8
    edges = [8 * (blocks * i // streams) for i in range(streams + 1)]
    parts = [(edges[i], edges[i + 1] - edges[i]) for i in range(streams)]
    whole_count = float(X * Y * Z * nd * nx * ny)
    R = WG + 8
    count = len(stages)
    dma = pltpu.SemaphoreType.DMA
    hidden, white, shift = pl.pallas_call(
        functools.partial(main_kernel, (nx, ny), tuple(stages), tuple(parts), whole_count),
        out_shape=(
            jax.ShapeDtypeStruct((X, Y * Z, C), BF16),
            jax.ShapeDtypeStruct((C, C), BF16),
            jax.ShapeDtypeStruct((8, C), F32),
        ),
        in_specs=[pl.BlockSpec(memory_space=pl.ANY), pl.BlockSpec(memory_space=pltpu.VMEM)],
        out_specs=(
            pl.BlockSpec(memory_space=pl.ANY),
            pl.BlockSpec(memory_space=pltpu.VMEM),
            pl.BlockSpec(memory_space=pltpu.VMEM),
        ),
        scratch_shapes=[
            pltpu.VMEM((X + 2, Y + 2, Z, 3 * C), BF16),
            pltpu.VMEM((27, C, C), BF16),
            pltpu.VMEM((X, Y * Z, C), F32),
            pltpu.VMEM((X, Y * Z, C), BF16),
            pltpu.VMEM((C + 8, C), F32),
            pltpu.VMEM((count + 1, R, WG), F32),
            pltpu.VMEM((count, R, WG), F32),
            pltpu.VMEM((R, WG), F32),
            pltpu.VMEM((R, WG), F32),
            pltpu.VMEM((R, WG), F32),
            pltpu.VMEM((R, WG), F32),
            dma, dma, dma((2,)), dma((2,)), dma((len(OTHERS),)), dma((len(OTHERS),)),
            dma((2,)), dma((2,)), dma((count, streams)), dma((count, streams)),
        ],
        compiler_params=pltpu.CompilerParams(
            collective_id=0, has_side_effects=True, vmem_limit_bytes=56 * 2**20),
        name="conv_moments",
    )(volume, kernel.reshape(27, GC, C))
    result = pl.pallas_call(
        apply_kernel,
        grid=(X // 2,),
        out_shape=jax.ShapeDtypeStruct((X, Y, Z, C), BF16),
        in_specs=[
            pl.BlockSpec((2, Y * Z, C), lambda i: (i, 0, 0)),
            pl.BlockSpec((C, C), lambda i: (0, 0)),
            pl.BlockSpec((8, C), lambda i: (0, 0)),
        ],
        out_specs=pl.BlockSpec((2, Y, Z, C), lambda i: (i, 0, 0, 0)),
        name="apply",
    )(hidden, white, shift)
    return result.reshape(volume.shape)


def solution(mesh):
    sizes = (mesh.shape["dp"], mesh.shape["sx"], mesh.shape["syz"])
    placed = (P("dp", "sx", "syz", None, None), P())
    return jax.shard_map(
        functools.partial(on_device, sizes),
        mesh=mesh,
        in_specs=placed,
        out_specs=P("dp", "sx", "syz", None, None),
        check_vma=False,
    )
```

```python
import functools

import jax
import jax.numpy as jnp
from jax import lax
from jax.experimental import pallas as pl
from jax.experimental.pallas import tpu as pltpu
from jax.sharding import PartitionSpec as P

WGROUPS = 2
STEPS = 5
epsilon = 1e-05
highest = lax.Precision.HIGHEST
MESH = pl.DeviceIdType.MESH
F32 = jnp.float32
BF16 = jnp.bfloat16
SIDES = (-1, 1)


def fma(a, b):
    return jnp.dot(a, b, preferred_element_type=F32)


def fdot(a, b):
    return jnp.dot(a, b, precision=highest, preferred_element_type=F32)


def main_kernel(
    sizes, stages, parts, whole_count,
    v_ref, k_ref, hid_out, white_ref, shift_ref,
    xs, wd, acc, hid, gram, red, got, give, got_pair, fin, got_fin,
    halo_y, halo_x, halo_c,
    load_sem, store_sem, send_y, recv_y, send_x, recv_x, send_c, recv_c,
    pair_send, pair_recv, tree_send, tree_recv,
):
    nx, ny = sizes
    X, Y, Z, C = v_ref.shape[1:]
    GC = k_ref.shape[1]
    WG = C // WGROUPS
    me_d = lax.axis_index("dp")
    me_x = lax.axis_index("sx")
    me_y = lax.axis_index("syz")

    def flip(axis, bit):
        me = lax.axis_index(axis)
        return {axis: me + bit - 2 * bit * ((me // bit) % 2)}

    def there(dx, dy):
        ok = None
        for d, me, n in ((dx, me_x, nx), (dy, me_y, ny)):
            if d:
                t = (me >= 1) if d < 0 else (me < n - 1)
                ok = t if ok is None else ok & t
        return ok

    def target(dx, dy):
        return (me_d, me_x + dx, me_y + dy)

    load = pltpu.make_async_copy(
        v_ref.at[0], xs.at[pl.ds(1, X), pl.ds(1, Y), :, pl.ds(C, C)], load_sem)
    load.start()

    barrier = pltpu.get_barrier_semaphore()
    near = ((0, -1), (0, 1), (-1, 0), (1, 0))
    for dx, dy in near:
        @pl.when(there(dx, dy))
        def _(dx=dx, dy=dy):
            pl.semaphore_signal(barrier, inc=1, device_id=target(dx, dy), device_id_type=MESH)
    far = [flip("dp", 1)] + [flip(a, b) for a, b in stages]
    for who in far:
        pl.semaphore_signal(barrier, inc=1, device_id=who, device_id_type=MESH)
    has_x = [jnp.where(there(d, 0), 1, 0) for d in (-1, 1)]
    has_y = [jnp.where(there(0, d), 1, 0) for d in (-1, 1)]
    around = has_x[0] + has_x[1] + has_y[0] + has_y[1]
    pl.semaphore_wait(barrier, around + len(far))

    def remote(src, dst, send, recv, dx, dy):
        return pltpu.make_async_remote_copy(
            src_ref=src, dst_ref=dst, send_sem=send, recv_sem=recv,
            device_id=target(dx, dy), device_id_type=MESH)

    def piece(x, side):
        d = SIDES[1 - side]
        return remote(v_ref.at[0, x, Y - 1 if d > 0 else 0], halo_y.at[side, x],
                      send_y.at[side, x], recv_y.at[side, x], 0, d)

    def face(side):
        d = SIDES[1 - side]
        return remote(v_ref.at[0, X - 1 if d > 0 else 0], halo_x.at[side],
                      send_x.at[side], recv_x.at[side], d, 0)

    def corner(side, side_y):
        d = SIDES[1 - side]
        return remote(halo_y.at[side_y, X - 1 if d > 0 else 0], halo_c.at[side, side_y],
                      send_c.at[side, side_y], recv_c.at[side, side_y], d, 0)

    early = [0] if X == 1 else [0, X - 1]
    order = early + list(range(1, X - 1))

    for x in early:
        for side in (0, 1):
            @pl.when(there(0, SIDES[1 - side]))
            def _(x=x, side=side):
                piece(x, side).start()
    for side in (0, 1):
        @pl.when(there(SIDES[1 - side], 0))
        def _(side=side):
            face(side).start()
    for x in order[len(early):]:
        for side in (0, 1):
            @pl.when(there(0, SIDES[1 - side]))
            def _(x=x, side=side):
                piece(x, side).start()

    for side in (0, 1):
        @pl.when(jnp.logical_not(there(0, SIDES[side])))
        def _(side=side):
            halo_y[side] = jnp.zeros((X, Z, C), BF16)

        @pl.when(jnp.logical_not(there(SIDES[side], 0)))
        def _(side=side):
            halo_x[side] = jnp.zeros((Y, Z, C), BF16)

        for side_y in (0, 1):
            @pl.when(jnp.logical_not(there(SIDES[side], SIDES[side_y])))
            def _(side=side, side_y=side_y):
                halo_c[side, side_y] = jnp.zeros((Z, C), BF16)

    lanes = lax.broadcasted_iota(jnp.int32, (GC, C), 1) // GC

    @pl.loop(0, k_ref.shape[0])
    def _(t):
        w = k_ref[t].astype(F32)
        for g in range(C // GC):
            wd[t, pl.ds(g * GC, GC), :] = jnp.where(lanes == g, w, 0.0).astype(BF16)

    rows = lax.broadcasted_iota(jnp.int32, (Z, C), 0)

    def shifted(px, py, source=None):
        v = xs[px, py, :, pl.ds(C, C)] if source is None else source
        if source is not None:
            xs[px, py, :, pl.ds(C, C)] = v
        v = v.astype(F32)
        xs[px, py, :, pl.ds(0, C)] = jnp.where(rows == 0, 0.0, pltpu.roll(v, 1, 0)).astype(BF16)
        xs[px, py, :, pl.ds(2 * C, C)] = jnp.where(
            rows == Z - 1, 0.0, pltpu.roll(v, Z - 1, 0)).astype(BF16)

    load.wait()

    @pl.loop(1, X + 1)
    def _(px):
        for py in range(1, Y + 1):
            shifted(px, py)

    def weight(a, b):
        return wd[pl.ds(((a + 1) * 3 + b + 1) * 3, 3)].reshape(3 * C, C)

    def inner(px, y0, n):
        return xs[px, pl.ds(y0, n)].reshape(n * Z, 3 * C)

    def taps(x, offsets):
        full = sum(fma(inner(x + 1 + a, 1, Y), weight(a, 0)) for a in offsets)
        if Y == 1:
            return full, None, None
        after = sum(fma(inner(x + 1 + a, 1, Y - 1), weight(a, -1)) for a in offsets)
        before = sum(fma(inner(x + 1 + a, 2, Y - 1), weight(a, 1)) for a in offsets)
        return full, after, before

    def plane(x, offsets, more=False):
        full, after, before = taps(x, offsets)
        if more:
            acc[x] += full
        else:
            acc[x] = full
        if Y > 1:
            m = (Y - 1) * Z
            acc[x, pl.ds(Z, m)] += after
            acc[x, pl.ds(0, m)] += before

    plane(0, (0, 1) if X > 1 else (0,))

    for x in early:
        for side_y in (0, 1):
            @pl.when(there(0, SIDES[side_y]))
            def _(x=x, side_y=side_y):
                piece(x, side_y).wait_recv()
    for side in (0, 1):
        for side_y in (0, 1):
            @pl.when(there(SIDES[1 - side], 0) & there(0, SIDES[side_y]))
            def _(side=side, side_y=side_y):
                corner(side, side_y).start()

    if X > 2:
        @pl.loop(1, X - 1)
        def _(x):
            plane(x, (-1, 0, 1))
    if X > 1:
        plane(X - 1, (-1, 0))

    for side in (0, 1):
        @pl.when(there(SIDES[side], 0))
        def _(side=side):
            face(side).wait_recv()
        for side_y in (0, 1):
            @pl.when(there(SIDES[side], SIDES[side_y]))
            def _(side=side, side_y=side_y):
                corner(side, side_y).wait_recv()
        px = (X + 1) * side

        @pl.loop(0, Y)
        def _(y, side=side, px=px):
            shifted(px, y + 1, halo_x[side, y])
        for side_y in (0, 1):
            shifted(px, (Y + 1) * side_y, halo_c[side, side_y])
    plane(0, (-1,), True)
    plane(X - 1, (1,), True)

    gram[...] = jnp.zeros_like(gram)
    for x in early:
        for side_y in (0, 1):
            shifted(x + 1, (Y + 1) * side_y, halo_y[side_y, x])
    pair_x = 2 if X % 2 == 0 else 1
    for x in range(0, X, pair_x):
        for new in range(x if x else 1, x + pair_x + 1):
            if (x == 0 or new > x) and new < X - 1:
                for side_y in (0, 1):
                    @pl.when(there(0, SIDES[side_y]))
                    def _(new=new, side_y=side_y):
                        piece(new, side_y).wait_recv()
                    shifted(new + 1, (Y + 1) * side_y, halo_y[side_y, new])
        for py, y, b in ((0, 0, -1), (Y + 1, Y - 1, 1)):
            add = sum(
                fma(xs[pl.ds(x + 1 + a, pair_x), py].reshape(pair_x * Z, 3 * C), weight(a, b))
                for a in (-1, 0, 1))
            acc[pl.ds(x, pair_x), pl.ds(y * Z, Z)] += add.reshape(pair_x, Z, C)
        h = acc[pl.ds(x, pair_x)].astype(BF16)
        hid[pl.ds(x, pair_x)] = h
        h = h.reshape(pair_x * Y * Z, C)
        gram[pl.ds(0, C)] += lax.dot_general(
            h, h, (((0,), (0,)), ((), ())), preferred_element_type=F32)
        gram[pl.ds(C, 8)] += jnp.sum(h.astype(F32).reshape(pair_x * Y * Z // 8, 8, C), axis=0)

    store = pltpu.make_async_copy(hid, hid_out, store_sem)
    store.start()

    mine = me_d == 0
    low = gram[pl.ds(0, WG), pl.ds(0, WG)]
    high = gram[pl.ds(WG, WG), pl.ds(WG, WG)]
    low_sum = gram[pl.ds(C, 8), pl.ds(0, WG)]
    high_sum = gram[pl.ds(C, 8), pl.ds(WG, WG)]
    give[pl.ds(0, WG)] = jnp.where(mine, high, low)
    give[pl.ds(WG, 8)] = jnp.where(mine, high_sum, low_sum)
    pair = flip("dp", 1)
    swap = pltpu.make_async_remote_copy(
        src_ref=give, dst_ref=got_pair, send_sem=pair_send.at[0], recv_sem=pair_recv.at[0],
        device_id=pair, device_id_type=MESH)
    swap.start()
    own = jnp.where(mine, low, high)
    own_sum = jnp.where(mine, low_sum, high_sum)
    swap.wait()
    red[0, pl.ds(0, WG)] = own + got_pair[pl.ds(0, WG)]
    red[0, pl.ds(WG, 8)] = own_sum + got_pair[pl.ds(WG, 8)]

    count = len(stages)

    def leg(step, stream):
        axis, bit = stages[(step + stream) % count]
        part = pl.ds(*parts[stream])
        return pltpu.make_async_remote_copy(
            src_ref=red.at[step, part], dst_ref=got.at[step, part],
            send_sem=tree_send.at[step, stream], recv_sem=tree_recv.at[step, stream],
            device_id=flip(axis, bit), device_id_type=MESH)

    for step in range(count):
        for stream in range(len(parts)):
            leg(step, stream).start()
        for stream in range(len(parts)):
            leg(step, stream).wait_recv()
            part = pl.ds(*parts[stream])
            red[step + 1, part] = red[step, part] + got[step, part]

    average = jnp.sum(red[count, pl.ds(WG, 8)], axis=0, keepdims=True) / whole_count
    across = jnp.broadcast_to(average, (WG, WG))
    down = across.T
    covariance = red[count, pl.ds(0, WG)] / whole_count - down * across
    identity = jnp.where(
        lax.broadcasted_iota(jnp.int32, (WG, WG), 0) == lax.broadcasted_iota(jnp.int32, (WG, WG), 1),
        1.0, 0.0).astype(F32)
    moved = covariance + epsilon * identity
    square = jnp.sum(jnp.sum(moved * moved, axis=1, keepdims=True), axis=0, keepdims=True)
    frobenius = jnp.sqrt(square)
    y = moved / frobenius
    z = None
    for number in range(STEPS):
        p = 1.5 * identity - 0.5 * (y if z is None else fdot(z, y))
        if number < STEPS - 1:
            y = fdot(y, p)
        z = p if z is None else fdot(p, z)
    whitener = z / jnp.sqrt(frobenius)
    turned = whitener.T.astype(BF16).astype(F32)
    fin[pl.ds(0, WG)] = turned
    fin[pl.ds(WG, 8)] = jnp.broadcast_to(jnp.sum(turned * down, axis=0, keepdims=True), (8, WG))
    swap = pltpu.make_async_remote_copy(
        src_ref=fin, dst_ref=got_fin, send_sem=pair_send.at[1], recv_sem=pair_recv.at[1],
        device_id=pair, device_id_type=MESH)
    swap.start()
    own = fin[...]
    swap.wait()
    other = got_fin[...]
    first = jnp.where(mine, own, other)
    second = jnp.where(mine, other, own)
    white_ref[...] = jnp.zeros_like(white_ref)
    white_ref[pl.ds(0, WG), pl.ds(0, WG)] = first[:WG].astype(BF16)
    white_ref[pl.ds(WG, WG), pl.ds(WG, WG)] = second[:WG].astype(BF16)
    shift_ref[:, pl.ds(0, WG)] = first[WG:]
    shift_ref[:, pl.ds(WG, WG)] = second[WG:]

    store.wait()
    for step in range(count):
        for stream in range(len(parts)):
            leg(step, stream).wait_send()
    for side in (0, 1):
        @pl.when(there(0, SIDES[1 - side]))
        def _(side=side):
            for x in range(X):
                piece(x, side).wait_send()

        @pl.when(there(SIDES[1 - side], 0))
        def _(side=side):
            face(side).wait_send()
        for side_y in (0, 1):
            @pl.when(there(SIDES[1 - side], 0) & there(0, SIDES[side_y]))
            def _(side=side, side_y=side_y):
                corner(side, side_y).wait_send()


def apply_kernel(h_ref, w_ref, s_ref, o_ref):
    X, M, C = h_ref.shape
    result = fma(h_ref[...].reshape(X * M, C), w_ref[...]) - s_ref[0:1, :]
    o_ref[...] = result.astype(BF16).reshape(o_ref.shape)


def on_device(sizes, volume, kernel):
    nd, nx, ny = sizes
    X, Y, Z, C = volume.shape[1:]
    GC = kernel.shape[3]
    WG = C // WGROUPS
    stages = []
    for axis, n in (("sx", nx), ("syz", ny)):
        bit = 1
        while bit < n:
            stages.append((axis, bit))
            bit *= 2
    streams = min(4, len(stages))
    blocks = (WG + 8) // 8
    edges = [8 * (blocks * i // streams) for i in range(streams + 1)]
    parts = [(edges[i], edges[i + 1] - edges[i]) for i in range(streams)]
    whole_count = float(X * Y * Z * nd * nx * ny)
    R = WG + 8
    count = len(stages)
    dma = pltpu.SemaphoreType.DMA
    hidden, white, shift = pl.pallas_call(
        functools.partial(main_kernel, (nx, ny), tuple(stages), tuple(parts), whole_count),
        out_shape=(
            jax.ShapeDtypeStruct((X, Y * Z, C), BF16),
            jax.ShapeDtypeStruct((C, C), BF16),
            jax.ShapeDtypeStruct((8, C), F32),
        ),
        in_specs=[pl.BlockSpec(memory_space=pl.ANY), pl.BlockSpec(memory_space=pltpu.VMEM)],
        out_specs=(
            pl.BlockSpec(memory_space=pl.ANY),
            pl.BlockSpec(memory_space=pltpu.VMEM),
            pl.BlockSpec(memory_space=pltpu.VMEM),
        ),
        scratch_shapes=[
            pltpu.VMEM((X + 2, Y + 2, Z, 3 * C), BF16),
            pltpu.VMEM((27, C, C), BF16),
            pltpu.VMEM((X, Y * Z, C), F32),
            pltpu.VMEM((X, Y * Z, C), BF16),
            pltpu.VMEM((C + 8, C), F32),
            pltpu.VMEM((count + 1, R, WG), F32),
            pltpu.VMEM((count, R, WG), F32),
            pltpu.VMEM((R, WG), F32),
            pltpu.VMEM((R, WG), F32),
            pltpu.VMEM((R, WG), F32),
            pltpu.VMEM((R, WG), F32),
            pltpu.VMEM((2, X, Z, C), BF16),
            pltpu.VMEM((2, Y, Z, C), BF16),
            pltpu.VMEM((2, 2, Z, C), BF16),
            dma, dma, dma((2, X)), dma((2, X)), dma((2,)), dma((2,)), dma((2, 2)), dma((2, 2)),
            dma((2,)), dma((2,)), dma((count, streams)), dma((count, streams)),
        ],
        compiler_params=pltpu.CompilerParams(
            collective_id=0, has_side_effects=True, vmem_limit_bytes=56 * 2**20),
        name="conv_moments",
    )(volume, kernel.reshape(27, GC, C))
    result = pl.pallas_call(
        apply_kernel,
        grid=(X // 2,),
        out_shape=jax.ShapeDtypeStruct((X, Y, Z, C), BF16),
        in_specs=[
            pl.BlockSpec((2, Y * Z, C), lambda i: (i, 0, 0)),
            pl.BlockSpec((C, C), lambda i: (0, 0)),
            pl.BlockSpec((8, C), lambda i: (0, 0)),
        ],
        out_specs=pl.BlockSpec((2, Y, Z, C), lambda i: (i, 0, 0, 0)),
        name="apply",
    )(hidden, white, shift)
    return result.reshape(volume.shape)


def solution(mesh):
    sizes = (mesh.shape["dp"], mesh.shape["sx"], mesh.shape["syz"])
    placed = (P("dp", "sx", "syz", None, None), P())
    return jax.shard_map(
        functools.partial(on_device, sizes),
        mesh=mesh,
        in_specs=placed,
        out_specs=P("dp", "sx", "syz", None, None),
        check_vma=False,
    )
```
